256 devices in a mesh: ctx: 32 (over z_hi, y, x), ch: 8 (over z_lo, core).
Axes of the slice: x: 4, y: 4, z: 8 (z_hi: 2, z_lo: 4; z = z_hi * 4 + z_lo), core: 2. Of those that a mesh axis runs over, the one named last changes fastest.
Arguments:
- grad_out: bfloat16 [24576, 4096], P('ctx', 'ch'), may hold values from -6 to 6
- block_input: bfloat16 [24576, 4096], P('ctx', 'ch'), may hold values from -40 to 40
- norm_gain: bfloat16 [4096], P('ch'), may hold values from 0.5 to 1.5
- queries: bfloat16 [24576, 4096], P('ctx', 'ch'), may hold values from -6 to 6
- keys: bfloat16 [24576, 4096], P('ctx', 'ch'), may hold values from -6 to 6
- values: bfloat16 [24576, 4096], P('ctx', 'ch'), may hold values from -6 to 6
- filters: bfloat16 [256, 128], P('ch'), may hold values from -0.5 to 0.5
- doc_starts: int32 [32, 4], P('ctx'), may hold values from 0 to 767, as said below
- in_weight: bfloat16 [4096, 3, 4096], P('ctx', None, 'ch'), may hold values from -0.09375 to 0.09375
- out_weight: bfloat16 [4096, 4096], P('ch', 'ctx'), may hold values from -0.09375 to 0.09375
Outputs:
- grad_input: bfloat16 [24576, 4096], P('ctx', 'ch')
The draws below stay inside these ranges and needn't reach their ends.
Inputs may be any that keep to these rules, and one draw needn't show every extreme that they name: `doc_starts`: each row holds 4 distinct document starts of one slab as offsets within the slab, in ascending order; the first slab's first start is 0.
All inputs are finite; a program needn't handle non-finite values.
Results may differ from the reference program's by a relative error of at most 0.013.
Values may be sent and summed in bfloat16 or wider, within the bound.
A program may use at most 128 MiB of HBM per device.

```python
import math
import jax
import jax.numpy as jnp
from jax import lax

D = 4096
FILTER_LEN = 128
GROUP_WIDTH = 16
DOCS = 4
TOK_DEV = 768
TOKENS = 24576
SLABS = 32
GROUPS = 256
CHAN_WIDTH = 512
N_CH = 8


def draw_block_input(key, part):
    first_key, second_key, third_key = jax.random.split(key, 3)
    row_scale = jnp.exp(jax.random.uniform(first_key, (TOKENS, 1), jnp.float32, math.log(0.3), math.log(3.0)))
    feature_pos = jnp.arange(D, dtype=jnp.float32) / D
    rising = math.log(3.0)
    base = jnp.clip(jax.random.normal(third_key, (TOKENS, D), jnp.float32), -3.5, 3.5)
    jitter = jax.random.uniform(second_key, (D,), jnp.float32, -0.5, 0.5)
    col_scale = jnp.exp(rising * (feature_pos - 0.5) + jitter)[None, :]
    return (base * row_scale * col_scale).astype(jnp.bfloat16)


def draw_doc_starts(key, part):
    slab_keys = jax.random.split(key, SLABS)

    def one_slab(slab_key):
        chosen = jax.random.permutation(slab_key, TOK_DEV - 1)[:DOCS] + 1
        return jnp.sort(chosen)
    starts = jax.vmap(one_slab)(slab_keys).astype(jnp.int32)
    starts = starts.at[0, 0].set(0)
    starts = starts.at[SLABS - 1, DOCS - 1].set(TOK_DEV - 1)
    return starts


def level_of(key, dims, cuts, least, high):
    level, own = 1.0, jax.random.fold_in(key, 6)
    for axis_at, shards_of in cuts:
        steps = jnp.exp(jax.random.uniform(jax.random.fold_in(own, axis_at), (shards_of,), jnp.float32, least / len(cuts), high / len(cuts)))
        level = level * jnp.repeat(steps, dims[axis_at] // shards_of).reshape([-1 if axis == axis_at else 1 for axis in range(len(dims))])
    return level


def noise(key, dims, width, limit, cuts=(), held_as=jnp.bfloat16):
    gain = level_of(key, dims, cuts, -0.22, 0.18) if cuts else 1.0
    entries = jax.random.normal(key, dims, jnp.float32) * width * gain
    return jnp.minimum(jnp.maximum(entries, -limit), limit).astype(held_as)


def setup_inputs(seed: int = 0) -> dict:
    arg_keys = jax.random.split(jax.random.key(seed), 11)
    return {
        "grad_out": noise(arg_keys[0], (TOKENS, D), 1.0, 6.0, ((0, 32), (1, 8))),
        "block_input": draw_block_input(jax.random.fold_in(arg_keys[10], 71), 0),
        "norm_gain": jnp.clip(1.0 + 0.1 * jax.random.normal(arg_keys[2], (D,), jnp.float32), 0.5, 1.5).astype(jnp.bfloat16),
        "queries": noise(arg_keys[3], (TOKENS, D), 1.0, 6.0, ((0, 32), (1, 8))),
        "keys": noise(arg_keys[4], (TOKENS, D), 1.0, 6.0, ((0, 32), (1, 8))),
        "values": noise(arg_keys[5], (TOKENS, D), 1.0, 6.0, ((0, 32), (1, 8))),
        "filters": noise(arg_keys[6], (GROUPS, FILTER_LEN), FILTER_LEN ** -0.5, 0.5, ((0, 8),)),
        "doc_starts": draw_doc_starts(jax.random.fold_in(arg_keys[10], 71), 0),
        "in_weight": noise(arg_keys[8], (D, 3, D), D ** -0.5, 0.09375, ((0, 32), (2, 8))),
        "out_weight": noise(arg_keys[9], (D, D), D ** -0.5, 0.09375, ((0, 8), (1, 32))),
    }


epsilon = 1e-05

def toeplitz_table(filters):
    tap_index = jnp.arange(FILTER_LEN, dtype=jnp.int32)[:, None] + FILTER_LEN - jnp.arange(2 * FILTER_LEN, dtype=jnp.int32)[None, :]
    valid = (tap_index >= 0) & (tap_index < FILTER_LEN)
    picked = jnp.take(filters.astype(jnp.float32), jnp.clip(tap_index, 0, FILTER_LEN - 1), axis=1)
    return jnp.where(valid[None], picked, jnp.float32(0.0))

def reference(grad_out, block_input, norm_gain, queries, keys, values, filters, doc_starts, in_weight, out_weight):
    slab_base = jnp.arange(SLABS, dtype=jnp.int32) * TOK_DEV
    starts = (doc_starts + slab_base[:, None]).reshape(-1).astype(jnp.int32)
    position = jnp.arange(TOKENS, dtype=jnp.int32)
    last_start = lax.optimization_barrier(jnp.max(jnp.where(starts[None, :] <= position[:, None], starts[None, :], -1), axis=1)).astype(jnp.int32)
    tile_count = TOKENS // FILTER_LEN
    table = toeplitz_table(filters)
    flipped = table[:, ::-1, ::-1]
    products = (keys.astype(jnp.float32) * values.astype(jnp.float32)).astype(jnp.bfloat16)
    padded_prod = jnp.concatenate([jnp.zeros((FILTER_LEN, D), jnp.bfloat16), products], axis=0)

    def forward_tile(tile_idx):
        source = lax.dynamic_slice_in_dim(padded_prod, tile_idx * FILTER_LEN, 2 * FILTER_LEN, 0)
        source = source.astype(jnp.float32).reshape(2 * FILTER_LEN, GROUPS, GROUP_WIDTH)
        row_last = lax.dynamic_slice_in_dim(last_start, tile_idx * FILTER_LEN, FILTER_LEN, 0)
        col_pos = (tile_idx - 1) * FILTER_LEN + jnp.arange(2 * FILTER_LEN, dtype=jnp.int32)
        allowed = col_pos[None, :] >= row_last[:, None]
        masked = jnp.where(allowed[None], table, jnp.float32(0.0))
        return jnp.einsum('gtp,pgc->tgc', masked, source).reshape(FILTER_LEN, D)
    mixed = lax.map(forward_tile, jnp.arange(tile_count, dtype=jnp.int32)).reshape(TOKENS, D)
    mix_grad = jnp.dot(grad_out, out_weight.T, preferred_element_type=jnp.float32)
    q_grad = (mix_grad * mixed).astype(jnp.bfloat16)
    w_grad = (mix_grad * queries.astype(jnp.float32)).astype(jnp.bfloat16)
    padded_grad = jnp.concatenate([w_grad, jnp.zeros((FILTER_LEN, D), jnp.bfloat16)], axis=0)
    padded_last = jnp.concatenate([last_start, jnp.full((FILTER_LEN,), TOKENS, jnp.int32)], axis=0)

    def backward_tile(tile_idx):
        source = lax.dynamic_slice_in_dim(padded_grad, tile_idx * FILTER_LEN, 2 * FILTER_LEN, 0)
        source = source.astype(jnp.float32).reshape(2 * FILTER_LEN, GROUPS, GROUP_WIDTH)
        col_last = lax.dynamic_slice_in_dim(padded_last, tile_idx * FILTER_LEN, 2 * FILTER_LEN, 0)
        row_pos = tile_idx * FILTER_LEN + jnp.arange(FILTER_LEN, dtype=jnp.int32)
        allowed = row_pos[:, None] >= col_last[None, :]
        masked = jnp.where(allowed[None], flipped, jnp.float32(0.0))
        return jnp.einsum('gst,tgc->sgc', masked, source).reshape(FILTER_LEN, D)
    conv_grad = lax.map(backward_tile, jnp.arange(tile_count, dtype=jnp.int32)).reshape(TOKENS, D)
    k_grad = (conv_grad * values.astype(jnp.float32)).astype(jnp.bfloat16)
    v_grad = (conv_grad * keys.astype(jnp.float32)).astype(jnp.bfloat16)
    stacked = jnp.stack([q_grad, k_grad, v_grad], axis=1)

    def group_step(running, group_idx):
        columns = lax.dynamic_slice_in_dim(stacked, group_idx * CHAN_WIDTH, CHAN_WIDTH, 2).reshape(TOKENS, 3 * CHAN_WIDTH)
        weight_part = lax.dynamic_slice_in_dim(in_weight, group_idx * CHAN_WIDTH, CHAN_WIDTH, 2).reshape(D, 3 * CHAN_WIDTH)
        partial_value = jnp.dot(columns, weight_part.T, preferred_element_type=jnp.float32).astype(jnp.bfloat16)
        partial_value = lax.optimization_barrier(partial_value)
        return (running + partial_value.astype(jnp.float32), None)
    norm_grad, unused = lax.scan(group_step, jnp.zeros((TOKENS, D), jnp.float32), jnp.arange(N_CH, dtype=jnp.int32))
    source_in = block_input.astype(jnp.float32)
    scaled = norm_gain.astype(jnp.float32)[None, :] * norm_grad
    square_sum = lax.optimization_barrier(jnp.sum(source_in * source_in, axis=1, keepdims=True))
    cross_sum = lax.optimization_barrier(jnp.sum(scaled * source_in, axis=1, keepdims=True))
    inverse = lax.rsqrt(square_sum / D + epsilon)
    result = grad_out.astype(jnp.float32) + inverse * scaled - source_in * (inverse * inverse * inverse) * cross_sum / D
    return result.astype(jnp.bfloat16)
```

```python
import functools

import jax
import jax.numpy as jnp
from jax import lax
from jax.experimental import pallas as pl
from jax.experimental.pallas import tpu as pltpu
from jax.sharding import PartitionSpec as P

D = 4096
LEN = 128
GROUP = 16
DOCS = 4
EPS = 1e-05
TOK = 768
CH = 512
TILES = TOK // LEN
BLOCKS = CH // 128
STACK = 128 // GROUP
F32 = jnp.float32
BF16 = jnp.bfloat16
NT = (((1,), (1,)), ((), ()))


def aligned(index, size):
    return pl.ds(pl.multiple_of(index * size, size), size)


def loop(count, body, start=0):
    def step(index, carry):
        body(index)
        return carry

    lax.fori_loop(start, count, step, 0)


def kernel(
    go_h, x_h, gain_v, q_h, k_h, v_h, filt_v, docs_v, iw_h, ow_h, out_h,
    grads, wts, ows, xin, qry, key, val, prod, wg, mixed, acc, stk, tabf, tabb, base, mask,
    docs, parts, sibs, runs, sums, fin, outv,
    lsem, ags, agr, bs, br, p0s, p0r, ws, wr, hs, hr, us, ur, ss, sr, cs, cr,
):
    ctx = lax.axis_index("ctx")
    ch = lax.axis_index("ch")
    x = ctx % 4
    y = (ctx // 4) % 4
    z = ctx // 16
    k = ch // 2
    core = ch % 2
    sib = 2 * k + 1 - core
    started = []

    def local(src, dst, index):
        return pltpu.make_async_copy(src, dst, lsem.at[index])

    def remote(src, dst, send, recv, to_ctx, to_ch):
        return pltpu.make_async_remote_copy(
            src, dst, send, recv, device_id=(to_ctx, to_ch), device_id_type=pl.DeviceIdType.MESH
        )

    def go(copy, cond=None):
        if cond is None:
            copy.start()
        else:
            pl.when(cond)(copy.start)
        started.append((copy, cond))

    def when(cond, body):
        pl.when(cond)(body)

    loads = [
        local(k_h, key, 0),
        local(v_h, val, 1),
        local(iw_h, wts.at[:, z, y, x], 2),
        local(ow_h, ows.at[z, y, x], 3),
        local(go_h, grads.at[ch], 4),
        local(x_h, xin, 5),
        local(q_h, qry, 6),
    ]
    for load in loads:
        load.start()

    barrier = pltpu.get_barrier_semaphore()
    up = (ctx + 1) % 32
    down = (ctx + 31) % 32

    def plane(dy, dx):
        return z * 16 + ((y + dy) % 4) * 4 + (x + dx) % 4

    partner = (1 - z) * 16 + y * 4 + x
    greet = [plane(0, 1), plane(0, 3), plane(1, 0), plane(3, 0), partner, up, down]
    for peer in greet:
        pl.semaphore_signal(barrier, inc=1, device_id=(peer, ch), device_id_type=pl.DeviceIdType.MESH)
    for step in range(1, 8):
        pl.semaphore_signal(
            barrier, inc=1, device_id=(ctx, (ch + step) % 8), device_id_type=pl.DeviceIdType.MESH
        )
    pl.semaphore_wait(barrier, len(greet) + 7)

    def piece(w, zi, yi, xi, quarter):
        if w == 0:
            return ows.at[zi, yi, xi, pl.ds(quarter * 128, 128), :]
        return wts.at[:, zi, yi, xi, pl.ds(quarter * 32, 32), :]

    def ring_copy(w, zz, quarter, step):
        zi = z if zz == 0 else 1 - z
        shift = 3 if quarter % 2 == 0 else 1
        along_y = (quarter < 2) == (step < 3)
        hop = 1 if quarter % 2 == 0 else 3
        peer = plane(hop, 0) if along_y else plane(0, hop)
        if step < 3:
            back = shift * step
            yi = (y + back) % 4 if along_y else y
            xi = x if along_y else (x + back) % 4
            dst = piece(w, zi, yi, xi, quarter)
            src = dst
            if step == 0 and zz == 0:
                if w == 0:
                    src = ow_h.at[pl.ds(quarter * 128, 128), :]
                else:
                    src = iw_h.at[:, pl.ds(quarter * 32, 32), :]
        else:
            back = shift * (step - 3)
            if along_y:
                yi, xi = (y + back) % 4, slice(None)
            else:
                yi, xi = slice(None), (x + back) % 4
            dst = piece(w, zi, yi, xi, quarter)
            src = dst
        return remote(src, dst, ws.at[w, zz, quarter, step], wr.at[w, zz, quarter, step], peer, ch)

    def ring_arrival(w, zz, quarter, step):
        zi = z if zz == 0 else 1 - z
        shift = 3 if quarter % 2 == 0 else 1
        along_y = (quarter < 2) == (step < 3)
        back = shift * (step % 3 + 1)
        if step < 3:
            yi = (y + back) % 4 if along_y else y
            xi = x if along_y else (x + back) % 4
        elif along_y:
            yi, xi = (y + back) % 4, slice(None)
        else:
            yi, xi = slice(None), (x + back) % 4
        dst = piece(w, zi, yi, xi, quarter)
        return remote(dst, dst, ws.at[w, zz, quarter, step], wr.at[w, zz, quarter, step], ctx, ch)

    def swap_copy(w):
        if w == 0:
            return remote(ow_h, ows.at[z, y, x], p0s.at[0], p0r.at[0], partner, ch)
        return remote(iw_h, wts.at[:, z, y, x], p0s.at[1], p0r.at[1], partner, ch)

    def swap_arrival(w):
        dst = ows.at[1 - z, y, x] if w == 0 else wts.at[:, 1 - z, y, x]
        return remote(dst, dst, p0s.at[w], p0r.at[w], ctx, ch)

    def weights(w, zz, event):
        if event == 0 and zz == 1:
            swap_arrival(w).wait_recv()
        if event == 3 and zz == 0:
            loads[3 - w].wait()
        for quarter in range(4):
            if event >= 1:
                ring_arrival(w, zz, quarter, event - 1).wait_recv()
            if event <= 5:
                go(ring_copy(w, zz, quarter, event))

    def line_copy(src_k, side, step):
        d = 2 * src_k + core
        to = (ch + 2) % 8 if side == 0 else (ch + 6) % 8
        src = go_h if step == 0 else grads.at[d]
        return remote(src, grads.at[d], ags.at[side, step], agr.at[src_k], ctx, to)

    def sib_copy(src_k, step):
        d = 2 * src_k + core
        src = go_h if step == 0 else grads.at[d]
        return remote(src, grads.at[d], bs.at[src_k], br.at[src_k], ctx, sib)

    def line_relay(step):
        for side, src_k, have, more in (
            (0, k - step, k >= step, k < 3),
            (1, k + step, k + step <= 3, k > 0),
        ):
            def relay(side=side, src_k=src_k, more=more):
                d = 2 * src_k + core
                remote(grads.at[d], grads.at[d], ags.at[side, step], agr.at[src_k], ctx, ch).wait_recv()
                if step < 3:
                    pl.when(more)(line_copy(src_k, side, step).start)
                sib_copy(src_k, step).start()

            when(have, relay)

    def multiply(d):
        zi, yi = d // 4, d % 4
        wide = jnp.concatenate([ows[zi, yi, xi] for xi in range(4)], axis=1)

        def rows_of(m):
            rows = aligned(m, 256)
            acc[rows, :] = acc[rows, :] + lax.dot_general(
                grads[d, rows, :], wide, NT, preferred_element_type=F32
            )

        loop(3, rows_of)

    def line_multiply(step):
        def one(index):
            side, other = index // 2, index % 2
            src_k = k - step + 2 * step * side

            def act():
                def await_sibling():
                    d = 2 * src_k + 1 - core
                    remote(grads.at[d], grads.at[d], bs.at[src_k], br.at[src_k], ctx, ch).wait_recv()

                when(other == 1, await_sibling)
                multiply(2 * src_k + core + other * (1 - 2 * core))

            when((src_k >= 0) & (src_k <= 3), act)

        loop(4, one)

    go(swap_copy(0))
    weights(0, 0, 0)
    go(line_copy(k, 0, 0), k < 3)
    go(line_copy(k, 1, 0), k > 0)
    go(sib_copy(k, 0))
    weights(1, 0, 0)
    go(swap_copy(1))
    wide_row = lax.broadcasted_iota(jnp.int32, (8, 2 * LEN), 0)
    own = jnp.zeros((8, 2 * LEN), jnp.int32)
    for i in range(DOCS):
        own = jnp.where(wide_row == i, docs_v[0:1, i : i + 1], own)
    docs[0] = own
    go(remote(docs.at[0], docs.at[1], hs.at[0], hr.at[0], up, ch))
    go(remote(docs.at[0], docs.at[2], hs.at[1], hr.at[1], down, ch))

    loads[0].wait()
    loads[1].wait()

    def product(i):
        rows = aligned(i, LEN)
        prod[pl.ds(pl.multiple_of(i * LEN + LEN, LEN), LEN), :] = (
            key[rows, :].astype(F32) * val[rows, :].astype(F32)
        ).astype(BF16)

    loop(TILES, product)
    go(remote(prod.at[pl.ds(TOK, LEN), :], prod.at[pl.ds(0, LEN), :], hs.at[2], hr.at[2], up, ch))
    weights(0, 0, 1)

    taps = filt_v[...]
    flip_row = lax.broadcasted_iota(jnp.int32, (LEN, 2 * LEN), 0)
    flip_col = lax.broadcasted_iota(jnp.int32, (LEN, 2 * LEN), 1)
    flip = jnp.where(flip_row + flip_col == LEN, 1.0, 0.0).astype(BF16)
    base[0] = jnp.dot(taps, flip, preferred_element_type=F32)
    base[1] = jnp.concatenate([taps.astype(F32), jnp.zeros((32, LEN), F32)], axis=1)

    def build(which, tab):
        def one(g):
            row = jnp.broadcast_to(base[which, pl.ds(g, 1), :], (LEN, 2 * LEN))
            tab[g] = pltpu.roll(row, 0, 1, stride=1, stride_axis=0).astype(BF16)

        loop(BLOCKS * STACK, one)

    build(0, tabf)
    weights(0, 1, 0)
    weights(1, 0, 1)

    loads[5].wait()

    def row_sums(i, which, wide):
        narrow = wide[:, 0:128] + wide[:, 128:256] + wide[:, 256:384] + wide[:, 384:512]
        sums[which, ch, pl.ds(i, 1), :] = jnp.sum(narrow.T, axis=0, keepdims=True)

    sums[0, ch] = jnp.zeros((8, 128), F32)
    sums[1, ch] = jnp.zeros((8, 128), F32)

    def squares(i):
        block = xin[aligned(i, LEN), :].astype(F32)
        row_sums(i, 0, block * block)

    loop(TILES, squares)

    def send_sums(which):
        for step in range(1, 8):
            to = (ch + step) % 8
            go(remote(sums.at[which, ch], sums.at[which, ch], us.at[which, step], ur.at[which, step], ctx, to))

    def await_sums(which):
        for step in range(1, 8):
            src = (ch + 8 - step) % 8
            remote(
                sums.at[which, src], sums.at[which, src], us.at[which, step], ur.at[which, step], ctx, ch
            ).wait_recv()

    send_sums(0)
    weights(0, 0, 2)
    weights(0, 1, 1)
    weights(1, 0, 2)
    build(1, tabb)
    weights(0, 0, 3)
    weights(0, 1, 2)
    weights(1, 0, 3)

    lane_group = lax.broadcasted_iota(jnp.int32, (LEN, 128), 1) // GROUP
    row_pos = lax.broadcasted_iota(jnp.int32, (LEN, 2 * LEN), 0)
    col_pos = lax.broadcasted_iota(jnp.int32, (LEN, 2 * LEN), 1)

    def set_mask(source, target, starts):
        cut = jnp.zeros((LEN, 2 * LEN), F32)
        for first in starts:
            cut = jnp.where((source < first) & (first <= target), 1.0, cut)
        mask[...] = (1.0 - cut).astype(BF16)

    def convolve(tab, src, i, b):
        lanes = aligned(b, 128)
        block = src[pl.ds(pl.multiple_of(i * LEN, LEN), 2 * LEN), lanes]
        left = (tab[pl.ds(pl.multiple_of(b * STACK, STACK), STACK)] * mask[...][None]).reshape(
            STACK * LEN, 2 * LEN
        )
        every = jnp.dot(left, block, preferred_element_type=F32).reshape(STACK, LEN, 128)
        picked = every[0]
        for g in range(1, STACK):
            picked = jnp.where(lane_group == g, every[g], picked)
        return picked

    def forward(i):
        set_mask(
            col_pos + (i * LEN - LEN),
            row_pos + i * LEN,
            [docs[0, r : r + 1, :] for r in range(DOCS)] + [docs[1, DOCS - 1 : DOCS, :] - TOK],
        )

        def one(b):
            mixed[aligned(i, LEN), aligned(b, 128)] = convolve(tabf, prod, i, b)

        loop(BLOCKS, one)

    remote(docs.at[0], docs.at[1], hs.at[0], hr.at[0], ctx, ch).wait_recv()
    loop(3, forward, 1)
    weights(0, 1, 3)
    weights(0, 0, 4)
    weights(1, 1, 0)
    loop(TILES, forward, 3)
    weights(0, 0, 5)
    weights(0, 1, 4)
    remote(prod.at[pl.ds(TOK, LEN), :], prod.at[pl.ds(0, LEN), :], hs.at[2], hr.at[2], ctx, ch).wait_recv()
    loop(1, forward)
    line_relay(1)
    weights(1, 0, 4)
    weights(0, 0, 6)
    weights(0, 1, 5)
    weights(0, 1, 6)
    weights(1, 1, 1)

    loads[4].wait()
    acc[...] = jnp.zeros((TOK, CH), F32)
    multiply(2 * k + core)
    remote(grads.at[sib], grads.at[sib], bs.at[k], br.at[k], ctx, ch).wait_recv()
    multiply(sib)
    line_multiply(1)
    weights(1, 0, 5)
    weights(1, 1, 2)
    line_relay(2)
    line_multiply(2)
    weights(1, 1, 3)
    weights(1, 0, 6)
    line_relay(3)
    line_multiply(3)
    weights(1, 1, 4)

    loads[6].wait()

    def gates(i):
        rows = aligned(i, LEN)
        mix = acc[rows, :]
        wg[rows, :] = (mix * qry[rows, :].astype(F32)).astype(BF16)
        stk[0, rows, :] = (mix * mixed[rows, :]).astype(BF16)

    loop(1, gates)
    go(remote(wg.at[pl.ds(0, LEN), :], wg.at[pl.ds(TOK, LEN), :], hs.at[3], hr.at[3], down, ch))
    loop(TILES, gates, 1)
    remote(docs.at[0], docs.at[2], hs.at[1], hr.at[1], ctx, ch).wait_recv()

    def backward(i):
        set_mask(
            row_pos + i * LEN,
            col_pos + i * LEN,
            [docs[0, r : r + 1, :] for r in range(DOCS)]
            + [docs[2, r : r + 1, :] + TOK for r in range(DOCS)],
        )

        def one(b):
            rows, lanes = aligned(i, LEN), aligned(b, 128)
            conv = convolve(tabb, wg, i, b)
            stk[1, rows, lanes] = (conv * val[rows, lanes].astype(F32)).astype(BF16)
            stk[2, rows, lanes] = (conv * key[rows, lanes].astype(F32)).astype(BF16)

        loop(BLOCKS, one)

    loop(TILES - 1, backward)
    weights(1, 1, 5)
    remote(wg.at[pl.ds(0, LEN), :], wg.at[pl.ds(TOK, LEN), :], hs.at[3], hr.at[3], ctx, ch).wait_recv()
    loop(TILES, backward, TILES - 1)
    weights(1, 1, 6)

    order = [3 * (1 - k // 2), (2 + 3 * k) % 5, 1 + k % 2, k]

    def partials(j):
        def one(part):
            d = 2 * j + (1 - core) * (1 - part) + core * part
            zi, yi = d // 4, d % 4

            def rows_of(m):
                rows = aligned(m, 256)
                total = lax.dot_general(
                    stk[0, rows, :], wts[0, zi, yi].reshape(CH, CH), NT, preferred_element_type=F32
                )
                for b in (1, 2):
                    total = total + lax.dot_general(
                        stk[b, rows, :], wts[b, zi, yi].reshape(CH, CH), NT, preferred_element_type=F32
                    )
                parts[part, j, rows, :] = total.astype(BF16)

            loop(3, rows_of)

            def send():
                remote(parts.at[0, j], sibs.at[j], ss.at[j], sr.at[j], ctx, sib).start()

            when(part == 0, send)

        loop(2, one)

    def await_sib(j):
        remote(parts.at[0, j], sibs.at[j], ss.at[j], sr.at[j], ctx, ch).wait_recv()

    def run_arrival(slot):
        remote(runs.at[slot], runs.at[slot], cs.at[0], cr.at[slot], ctx, ch).wait_recv()

    def chain_copy(j, side):
        to = (ch + 2) % 8 if side == 0 else (ch + 6) % 8
        slot = j + 4 * side
        return remote(parts.at[1, j], runs.at[slot], cs.at[j], cr.at[slot], ctx, to)

    def forward_sum(j):
        await_sib(j)
        inner = (k == 1) | (k == 2)
        slot = j + 4 * ((k - j + 3) // 4)

        def with_run():
            run_arrival(slot)

            def add(i):
                rows = aligned(i, LEN)
                parts[1, j, rows, :] = (
                    parts[1, j, rows, :].astype(F32)
                    + sibs[j, rows, :].astype(F32)
                    + runs[slot, rows, :].astype(F32)
                ).astype(BF16)

            loop(TILES, add)

        def without_run():
            def add(i):
                rows = aligned(i, LEN)
                parts[1, j, rows, :] = (
                    parts[1, j, rows, :].astype(F32) + sibs[j, rows, :].astype(F32)
                ).astype(BF16)

            loop(TILES, add)

        when(inner, with_run)
        when(jnp.logical_not(inner), without_run)
        when(j > k, chain_copy(j, 0).start)
        when(j < k, chain_copy(j, 1).start)

    def clear(slot):
        def one():
            runs[slot] = jnp.zeros((TOK, CH), BF16)

        return one

    when(k == 0, clear(0))
    when(k == 3, clear(7))
    partials(order[0])
    partials(order[1])
    forward_sum(order[0])
    forward_sum(order[1])
    partials(order[2])
    forward_sum(order[2])
    partials(order[3])
    await_sib(k)
    when(k > 0, lambda: run_arrival(k))
    when(k < 3, lambda: run_arrival(4 + k))

    gain = gain_v[...].astype(F32)

    def cross(i):
        rows = aligned(i, LEN)
        norm = (
            parts[1, k, rows, :].astype(F32)
            + sibs[k, rows, :].astype(F32)
            + runs[k, rows, :].astype(F32)
            + runs[4 + k, rows, :].astype(F32)
        )
        scaled = gain * norm
        acc[rows, :] = scaled
        row_sums(i, 1, scaled * xin[rows, :].astype(F32))

    loop(TILES, cross)
    send_sums(1)
    await_sums(0)
    await_sums(1)

    def total(which):
        full = sums[which, 0]
        for src in range(1, 8):
            full = full + sums[which, src]
        return full

    fin[0] = lax.rsqrt(total(0) / D + EPS)
    fin[1] = total(1) / D

    def column(row):
        tall = jnp.broadcast_to(row, (128, 128)).T
        return jnp.concatenate([tall] * BLOCKS, axis=1)

    def finish(i):
        rows = aligned(i, LEN)
        inverse = column(fin[0, pl.ds(i, 1), :])
        crossed = column(fin[1, pl.ds(i, 1), :])
        outv[rows, :] = (
            grads[ch, rows, :].astype(F32)
            + inverse * acc[rows, :]
            - xin[rows, :].astype(F32) * (inverse * inverse * inverse) * crossed
        ).astype(BF16)

    loop(TILES, finish)
    store = local(outv, out_h, 7)
    store.start()

    for copy, cond in started:
        if cond is None:
            copy.wait_send()
        else:
            pl.when(cond)(copy.wait_send)
    for step in (1, 2, 3):
        for side, src_k, have, more in (
            (0, k - step, k >= step, k < 3),
            (1, k + step, k + step <= 3, k > 0),
        ):
            def drain(side=side, src_k=src_k, more=more):
                if step < 3:
                    pl.when(more)(line_copy(src_k, side, step).wait_send)
                sib_copy(src_k, step).wait_send()

            when(have, drain)
    for j in order:
        remote(parts.at[0, j], sibs.at[j], ss.at[j], sr.at[j], ctx, sib).wait_send()
        when(j > k, chain_copy(j, 0).wait_send)
        when(j < k, chain_copy(j, 1).wait_send)
    store.wait()


def on_device(
    grad_out, block_input, norm_gain, queries, keys, values, filters, doc_starts, in_weight, out_weight
):
    hbm = pl.BlockSpec(memory_space=pl.ANY)
    vmem = pl.BlockSpec(memory_space=pltpu.VMEM)
    dma = pltpu.SemaphoreType.DMA
    return pl.pallas_call(
        kernel,
        out_shape=jax.ShapeDtypeStruct((TOK, CH), BF16),
        in_specs=[hbm, hbm, vmem, hbm, hbm, hbm, vmem, vmem, hbm, hbm],
        out_specs=hbm,
        scratch_shapes=[
            pltpu.VMEM((8, TOK, CH), BF16),
            pltpu.VMEM((3, 2, 4, 4, 128, CH), BF16),
            pltpu.VMEM((2, 4, 4, CH, 128), BF16),
            pltpu.VMEM((TOK, CH), BF16),
            pltpu.VMEM((TOK, CH), BF16),
            pltpu.VMEM((TOK, CH), BF16),
            pltpu.VMEM((TOK, CH), BF16),
            pltpu.VMEM((TOK + LEN, CH), BF16),
            pltpu.VMEM((TOK + LEN, CH), BF16),
            pltpu.VMEM((TOK, CH), F32),
            pltpu.VMEM((TOK, CH), F32),
            pltpu.VMEM((3, TOK, CH), BF16),
            pltpu.VMEM((32, LEN, 2 * LEN), BF16),
            pltpu.VMEM((32, LEN, 2 * LEN), BF16),
            pltpu.VMEM((2, 32, 2 * LEN), F32),
            pltpu.VMEM((LEN, 2 * LEN), BF16),
            pltpu.VMEM((3, 8, 2 * LEN), jnp.int32),
            pltpu.VMEM((2, 4, TOK, CH), BF16),
            pltpu.VMEM((4, TOK, CH), BF16),
            pltpu.VMEM((8, TOK, CH), BF16),
            pltpu.VMEM((2, 8, 8, 128), F32),
            pltpu.VMEM((2, 8, 128), F32),
            pltpu.VMEM((TOK, CH), BF16),
            dma((8,)),
            dma((2, 3)),
            dma((4,)),
            dma((4,)),
            dma((4,)),
            dma((2,)),
            dma((2,)),
            dma((2, 2, 4, 6)),
            dma((2, 2, 4, 6)),
            dma((4,)),
            dma((4,)),
            dma((2, 8)),
            dma((2, 8)),
            dma((4,)),
            dma((4,)),
            dma((4,)),
            dma((8,)),
        ],
        compiler_params=pltpu.CompilerParams(
            collective_id=0, has_side_effects=True, vmem_limit_bytes=66 * 1024 * 1000
        ),
    )(
        grad_out,
        block_input,
        norm_gain.reshape(1, -1),
        queries,
        keys,
        values,
        filters,
        doc_starts,
        jnp.transpose(in_weight, (1, 0, 2)),
        out_weight,
    )


def solution(mesh):
    placed = (
        P("ctx", "ch"),
        P("ctx", "ch"),
        P("ch"),
        P("ctx", "ch"),
        P("ctx", "ch"),
        P("ctx", "ch"),
        P("ch", None),
        P("ctx", None),
        P("ctx", None, "ch"),
        P("ch", "ctx"),
    )
    return jax.shard_map(
        on_device, mesh=mesh, in_specs=placed, out_specs=P("ctx", "ch"), check_vma=False
    )
```

```python
import functools

import jax
import jax.numpy as jnp
from jax import lax
from jax.experimental import pallas as pl
from jax.experimental.pallas import tpu as pltpu
from jax.sharding import PartitionSpec as P

D = 4096
LEN = 128
GROUP = 16
DOCS = 4
EPS = 1e-05
TOK = 768
CH = 512
TILES = TOK // LEN
BLOCKS = CH // 128
STACK = 128 // GROUP
F32 = jnp.float32
BF16 = jnp.bfloat16
NT = (((1,), (1,)), ((), ()))


def aligned(index, size):
    return pl.ds(index * size if isinstance(index, int) else pl.multiple_of(index * size, size), size)


def loop(count, body, start=0):
    def step(index, carry):
        body(index)
        return carry

    lax.fori_loop(start, count, step, 0)


def kernel(
    go_h, x_h, gain_v, q_h, k_h, v_h, filt_v, docs_v, iw_h, ow_h, out_h,
    grads, wts, ows, xin, qry, key, val, prod, wg, mixed, acc, stk, tabf, tabb, base, mask,
    docs, parts, sibs, runs, sums, fin, outv,
    lsem, ags, agr, bs, br, p0s, p0r, ws, wr, hs, hr, us, ur, ss, sr, cs, cr,
):
    ctx = lax.axis_index("ctx")
    ch = lax.axis_index("ch")
    x = ctx % 4
    y = (ctx // 4) % 4
    z = ctx // 16
    k = ch // 2
    core = ch % 2
    sib = 2 * k + 1 - core
    started = []

    def local(src, dst, index):
        return pltpu.make_async_copy(src, dst, lsem.at[index])

    def remote(src, dst, send, recv, to_ctx, to_ch):
        return pltpu.make_async_remote_copy(
            src, dst, send, recv, device_id=(to_ctx, to_ch), device_id_type=pl.DeviceIdType.MESH
        )

    def go(copy, cond=None):
        if cond is None:
            copy.start()
        else:
            pl.when(cond)(copy.start)
        started.append((copy, cond))

    def when(cond, body):
        pl.when(cond)(body)

    loads = [
        local(k_h, key, 0),
        local(v_h, val, 1),
        local(iw_h, wts.at[:, z, y, x], 2),
        local(ow_h, ows.at[z, y, x], 3),
        local(go_h, grads.at[ch], 4),
        local(x_h, xin, 5),
        local(q_h, qry, 6),
    ]
    for load in loads:
        load.start()

    barrier = pltpu.get_barrier_semaphore()
    up = (ctx + 1) % 32
    down = (ctx + 31) % 32

    def plane(dy, dx):
        return z * 16 + ((y + dy) % 4) * 4 + (x + dx) % 4

    partner = (1 - z) * 16 + y * 4 + x
    greet = [plane(0, 1), plane(0, 3), plane(1, 0), plane(3, 0), partner, up, down]
    for peer in greet:
        pl.semaphore_signal(barrier, inc=1, device_id=(peer, ch), device_id_type=pl.DeviceIdType.MESH)
    for step in range(1, 8):
        pl.semaphore_signal(
            barrier, inc=1, device_id=(ctx, (ch + step) % 8), device_id_type=pl.DeviceIdType.MESH
        )
    wide_row = lax.broadcasted_iota(jnp.int32, (8, 2 * LEN), 0)
    own = jnp.zeros((8, 2 * LEN), jnp.int32)
    for i in range(DOCS):
        own = jnp.where(wide_row == i, docs_v[0:1, i : i + 1], own)
    docs[0] = own

    loads[0].wait()
    loads[1].wait()

    def product(i):
        rows = aligned(i, LEN)
        prod[pl.ds(pl.multiple_of(i * LEN + LEN, LEN), LEN), :] = (
            key[rows, :].astype(F32) * val[rows, :].astype(F32)
        ).astype(BF16)

    loop(TILES, product)

    taps = filt_v[...]
    flip_row = lax.broadcasted_iota(jnp.int32, (LEN, 2 * LEN), 0)
    flip_col = lax.broadcasted_iota(jnp.int32, (LEN, 2 * LEN), 1)
    flip = jnp.where(flip_row + flip_col == LEN, 1.0, 0.0).astype(BF16)
    base[0] = jnp.dot(taps, flip, preferred_element_type=F32)
    base[1] = jnp.concatenate([taps.astype(F32), jnp.zeros((32, LEN), F32)], axis=1)

    def build(which, tab):
        def one(g):
            row = jnp.broadcast_to(base[which, pl.ds(g, 1), :], (LEN, 2 * LEN))
            tab[g] = pltpu.roll(row, 0, 1, stride=1, stride_axis=0).astype(BF16)

        loop(BLOCKS * STACK, one)

    build(0, tabf)

    loads[5].wait()

    def row_sums(i, which, wide):
        narrow = wide[:, 0:128] + wide[:, 128:256] + wide[:, 256:384] + wide[:, 384:512]
        sums[which, ch, pl.ds(i, 1), :] = jnp.sum(narrow.T, axis=0, keepdims=True)

    sums[0, ch] = jnp.zeros((8, 128), F32)
    sums[1, ch] = jnp.zeros((8, 128), F32)

    def squares(i):
        block = xin[aligned(i, LEN), :].astype(F32)
        row_sums(i, 0, block * block)

    loop(TILES, squares)

    pl.semaphore_wait(barrier, len(greet) + 7)

    def piece(w, zi, yi, xi, quarter):
        if w == 0:
            return ows.at[zi, yi, xi, pl.ds(quarter * 128, 128), :]
        return wts.at[:, zi, yi, xi, pl.ds(quarter * 32, 32), :]

    def ring_copy(w, zz, quarter, step):
        zi = z if zz == 0 else 1 - z
        shift = 3 if quarter % 2 == 0 else 1
        along_y = (quarter < 2) == (step < 3)
        hop = 1 if quarter % 2 == 0 else 3
        peer = plane(hop, 0) if along_y else plane(0, hop)
        if step < 3:
            back = shift * step
            yi = (y + back) % 4 if along_y else y
            xi = x if along_y else (x + back) % 4
            dst = piece(w, zi, yi, xi, quarter)
            src = dst
            if step == 0 and zz == 0:
                if w == 0:
                    src = ow_h.at[pl.ds(quarter * 128, 128), :]
                else:
                    src = iw_h.at[:, pl.ds(quarter * 32, 32), :]
        else:
            back = shift * (step - 3)
            if along_y:
                yi, xi = (y + back) % 4, slice(None)
            else:
                yi, xi = slice(None), (x + back) % 4
            dst = piece(w, zi, yi, xi, quarter)
            src = dst
        return remote(src, dst, ws.at[w, zz, quarter, step], wr.at[w, zz, quarter, step], peer, ch)

    def ring_arrival(w, zz, quarter, step):
        zi = z if zz == 0 else 1 - z
        shift = 3 if quarter % 2 == 0 else 1
        along_y = (quarter < 2) == (step < 3)
        back = shift * (step % 3 + 1)
        if step < 3:
            yi = (y + back) % 4 if along_y else y
            xi = x if along_y else (x + back) % 4
        elif along_y:
            yi, xi = (y + back) % 4, slice(None)
        else:
            yi, xi = slice(None), (x + back) % 4
        dst = piece(w, zi, yi, xi, quarter)
        return remote(dst, dst, ws.at[w, zz, quarter, step], wr.at[w, zz, quarter, step], ctx, ch)

    def swap_copy(w):
        if w == 0:
            return remote(ow_h, ows.at[z, y, x], p0s.at[0], p0r.at[0], partner, ch)
        return remote(iw_h, wts.at[:, z, y, x], p0s.at[1], p0r.at[1], partner, ch)

    def swap_arrival(w):
        dst = ows.at[1 - z, y, x] if w == 0 else wts.at[:, 1 - z, y, x]
        return remote(dst, dst, p0s.at[w], p0r.at[w], ctx, ch)

    def weights(w, zz, event):
        if event == 0 and zz == 1:
            swap_arrival(w).wait_recv()
        if event == 3 and zz == 0:
            loads[3 - w].wait()
        for quarter in range(4):
            if event >= 1:
                ring_arrival(w, zz, quarter, event - 1).wait_recv()
            if event <= 5:
                go(ring_copy(w, zz, quarter, event))

    def line_copy(src_k, side, step):
        d = 2 * src_k + core
        to = (ch + 2) % 8 if side == 0 else (ch + 6) % 8
        src = go_h if step == 0 else grads.at[d]
        return remote(src, grads.at[d], ags.at[side, step], agr.at[src_k], ctx, to)

    def sib_copy(src_k, step):
        d = 2 * src_k + core
        src = go_h if step == 0 else grads.at[d]
        return remote(src, grads.at[d], bs.at[src_k], br.at[src_k], ctx, sib)

    def line_relay(step):
        for side, src_k, have, more in (
            (0, k - step, k >= step, k < 3),
            (1, k + step, k + step <= 3, k > 0),
        ):
            def relay(side=side, src_k=src_k, more=more):
                d = 2 * src_k + core
                remote(grads.at[d], grads.at[d], ags.at[side, step], agr.at[src_k], ctx, ch).wait_recv()
                if step < 3:
                    pl.when(more)(line_copy(src_k, side, step).start)
                sib_copy(src_k, step).start()

            when(have, relay)

    def multiply(d):
        zi, yi = d // 4, d % 4
        wide = jnp.concatenate([ows[zi, yi, xi] for xi in range(4)], axis=1)

        def rows_of(m):
            rows = aligned(m, 256)
            acc[rows, :] = acc[rows, :] + lax.dot_general(
                grads[d, rows, :], wide, NT, preferred_element_type=F32
            )

        loop(3, rows_of)

    def line_multiply(step):
        def one(index):
            side, other = index // 2, index % 2
            src_k = k - step + 2 * step * side

            def act():
                def await_sibling():
                    d = 2 * src_k + 1 - core
                    remote(grads.at[d], grads.at[d], bs.at[src_k], br.at[src_k], ctx, ch).wait_recv()

                when(other == 1, await_sibling)
                multiply(2 * src_k + core + other * (1 - 2 * core))

            when((src_k >= 0) & (src_k <= 3), act)

        loop(4, one)

    go(remote(docs.at[0], docs.at[1], hs.at[0], hr.at[0], up, ch))
    go(remote(docs.at[0], docs.at[2], hs.at[1], hr.at[1], down, ch))
    weights(0, 0, 0)
    weights(1, 0, 0)
    go(remote(prod.at[pl.ds(TOK, LEN), :], prod.at[pl.ds(0, LEN), :], hs.at[2], hr.at[2], up, ch))
    go(swap_copy(0))
    go(swap_copy(1))
    go(line_copy(k, 0, 0), k < 3)
    go(line_copy(k, 1, 0), k > 0)
    go(sib_copy(k, 0))

    def send_sums(which):
        for step in range(1, 8):
            to = (ch + step) % 8
            go(remote(sums.at[which, ch], sums.at[which, ch], us.at[which, step], ur.at[which, step], ctx, to))

    def await_sums(which):
        for step in range(1, 8):
            src = (ch + 8 - step) % 8
            remote(
                sums.at[which, src], sums.at[which, src], us.at[which, step], ur.at[which, step], ctx, ch
            ).wait_recv()

    send_sums(0)

    lane_group = lax.broadcasted_iota(jnp.int32, (LEN, 128), 1) // GROUP
    row_pos = lax.broadcasted_iota(jnp.int32, (LEN, 2 * LEN), 0)
    col_pos = lax.broadcasted_iota(jnp.int32, (LEN, 2 * LEN), 1)

    def set_mask(source, target, starts):
        cut = jnp.zeros((LEN, 2 * LEN), F32)
        for first in starts:
            cut = jnp.where((source < first) & (first <= target), 1.0, cut)
        mask[...] = (1.0 - cut).astype(BF16)

    def convolve(tab, src, i, b):
        lanes = aligned(b, 128)
        first = i * LEN if isinstance(i, int) else pl.multiple_of(i * LEN, LEN)
        block = src[pl.ds(first, 2 * LEN), lanes]
        left = (tab[pl.ds(pl.multiple_of(b * STACK, STACK), STACK)] * mask[...][None]).reshape(
            STACK * LEN, 2 * LEN
        )
        every = jnp.dot(left, block, preferred_element_type=F32).reshape(STACK, LEN, 128)
        picked = every[0]
        for g in range(1, STACK):
            picked = jnp.where(lane_group == g, every[g], picked)
        return picked

    def forward(i):
        firsts = [docs[0, r : r + 1, :] for r in range(DOCS)]
        if isinstance(i, int):
            firsts.append(docs[1, DOCS - 1 : DOCS, :] - TOK)
        set_mask(col_pos + (i * LEN - LEN), row_pos + i * LEN, firsts)

        def one(b):
            mixed[aligned(i, LEN), aligned(b, 128)] = convolve(tabf, prod, i, b)

        loop(BLOCKS, one)

    for event in (1, 2, 3):
        weights(0, 0, event)
        weights(1, 0, event)
    loop(TILES, forward, 3)
    weights(0, 1, 0)
    weights(0, 0, 4)
    weights(0, 1, 1)
    weights(1, 0, 4)
    weights(1, 1, 0)
    weights(0, 0, 5)
    weights(0, 1, 2)
    line_relay(1)
    weights(1, 1, 1)
    weights(0, 1, 3)
    weights(1, 1, 2)
    weights(0, 1, 4)
    build(1, tabb)
    weights(1, 1, 3)
    loop(3, forward, 1)
    remote(prod.at[pl.ds(TOK, LEN), :], prod.at[pl.ds(0, LEN), :], hs.at[2], hr.at[2], ctx, ch).wait_recv()
    remote(docs.at[0], docs.at[1], hs.at[0], hr.at[0], ctx, ch).wait_recv()
    forward(0)
    line_relay(2)
    weights(0, 1, 5)
    weights(1, 1, 4)
    weights(0, 1, 6)
    weights(0, 0, 6)
    loads[4].wait()
    acc[...] = jnp.zeros((TOK, CH), F32)
    multiply(2 * k + core)
    remote(grads.at[sib], grads.at[sib], bs.at[k], br.at[k], ctx, ch).wait_recv()
    multiply(sib)
    weights(1, 0, 5)
    line_multiply(1)
    line_relay(3)
    line_multiply(2)
    weights(1, 1, 5)
    line_multiply(3)

    loads[6].wait()

    def gates(i):
        rows = aligned(i, LEN)
        mix = acc[rows, :]
        wg[rows, :] = (mix * qry[rows, :].astype(F32)).astype(BF16)
        stk[0, rows, :] = (mix * mixed[rows, :]).astype(BF16)

    loop(1, gates)
    go(remote(wg.at[pl.ds(0, LEN), :], wg.at[pl.ds(TOK, LEN), :], hs.at[3], hr.at[3], down, ch))
    loop(TILES, gates, 1)
    remote(docs.at[0], docs.at[2], hs.at[1], hr.at[1], ctx, ch).wait_recv()

    def backward(i):
        set_mask(
            row_pos + i * LEN,
            col_pos + i * LEN,
            [docs[0, r : r + 1, :] for r in range(DOCS)]
            + [docs[2, r : r + 1, :] + TOK for r in range(DOCS)],
        )

        def one(b):
            rows, lanes = aligned(i, LEN), aligned(b, 128)
            conv = convolve(tabb, wg, i, b)
            stk[1, rows, lanes] = (conv * val[rows, lanes].astype(F32)).astype(BF16)
            stk[2, rows, lanes] = (conv * key[rows, lanes].astype(F32)).astype(BF16)

        loop(BLOCKS, one)

    loop(TILES - 1, backward)
    weights(1, 0, 6)
    remote(wg.at[pl.ds(0, LEN), :], wg.at[pl.ds(TOK, LEN), :], hs.at[3], hr.at[3], ctx, ch).wait_recv()
    loop(TILES, backward, TILES - 1)
    weights(1, 1, 6)

    order = [3 * (1 - k // 2), (2 + 3 * k) % 5, 1 + k % 2, k]

    def target(pos):
        return sum(order[i] * ((4 - (pos + 4 - i) % 4) // 4) for i in range(4))

    def chunk(c):
        return aligned(c, 256)

    def sib_part(j, c, to):
        rows = chunk(c)
        return remote(parts.at[0, j, rows], sibs.at[j, rows], ss.at[j, c], sr.at[j, c], ctx, to)

    def run_arrival(slot, c):
        rows = chunk(c)
        remote(runs.at[slot, rows], runs.at[slot, rows], cs.at[0, c], cr.at[slot, c], ctx, ch).wait_recv()

    def chain_copy(j, c, side):
        rows = chunk(c)
        to = (ch + 2) % 8 if side == 0 else (ch + 6) % 8
        slot = j + 4 * side
        return remote(parts.at[1, j, rows], runs.at[slot, rows], cs.at[j, c], cr.at[slot, c], ctx, to)

    def partials(j, c):
        rows = chunk(c)

        def one(part):
            d = 2 * j + (1 - core) * (1 - part) + core * part
            zi, yi = d // 4, d % 4
            total = lax.dot_general(
                stk[0, rows, :], wts[0, zi, yi].reshape(CH, CH), NT, preferred_element_type=F32
            )
            for b in (1, 2):
                total = total + lax.dot_general(
                    stk[b, rows, :], wts[b, zi, yi].reshape(CH, CH), NT, preferred_element_type=F32
                )
            parts[part, j, rows, :] = total.astype(BF16)
            when(part == 0, sib_part(j, c, sib).start)

        loop(2, one)

    def forward_sum(j, c):
        sib_part(j, c, ch).wait_recv()
        inner = (k == 1) | (k == 2)
        slot = j + 4 * ((k - j + 3) // 4)

        def pieces(i):
            return pl.ds(pl.multiple_of(c * 256 + i * 64, 64), 64)

        def with_run():
            run_arrival(slot, c)

            def add(i):
                rows = pieces(i)
                parts[1, j, rows, :] = (
                    parts[1, j, rows, :].astype(F32)
                    + sibs[j, rows, :].astype(F32)
                    + runs[slot, rows, :].astype(F32)
                ).astype(BF16)

            loop(4, add)

        def without_run():
            def add(i):
                rows = pieces(i)
                parts[1, j, rows, :] = (
                    parts[1, j, rows, :].astype(F32) + sibs[j, rows, :].astype(F32)
                ).astype(BF16)

            loop(4, add)

        when(inner, with_run)
        when(jnp.logical_not(inner), without_run)
        when(j > k, chain_copy(j, c, 0).start)
        when(j < k, chain_copy(j, c, 1).start)

    def clear(slot):
        def one():
            runs[slot] = jnp.zeros((TOK, CH), BF16)

        return one

    when(k == 0, clear(0))
    when(k == 3, clear(7))

    def job(n):
        partials(target(n // 3), n % 3)
        done = n - 2

        def behind():
            forward_sum(target(done // 3), done % 3)

        when((done >= 0) & (done < 9), behind)

    loop(12, job)

    def total(which):
        full = sums[which, 0]
        for src in range(1, 8):
            full = full + sums[which, src]
        return full

    def column(row):
        tall = jnp.broadcast_to(row, (128, 128)).T
        return jnp.concatenate([tall] * BLOCKS, axis=1)

    await_sums(0)
    fin[0] = lax.rsqrt(total(0) / D + EPS)
    gain = gain_v[...].astype(F32)

    def cross(i):
        rows = aligned(i, LEN)
        norm = (
            parts[1, k, rows, :].astype(F32)
            + sibs[k, rows, :].astype(F32)
            + runs[k, rows, :].astype(F32)
            + runs[4 + k, rows, :].astype(F32)
        )
        scaled = gain * norm
        acc[rows, :] = scaled
        row_sums(i, 1, scaled * xin[rows, :].astype(F32))

    for c in range(3):
        sib_part(k, c, ch).wait_recv()
        when(k > 0, functools.partial(run_arrival, k, c))
        when(k < 3, functools.partial(run_arrival, 4 + k, c))
        loop(2 * c + 2, cross, 2 * c)
    send_sums(1)

    def prepare(i):
        rows = aligned(i, LEN)
        inverse = column(fin[0, pl.ds(i, 1), :])
        acc[rows, :] = grads[ch, rows, :].astype(F32) + inverse * acc[rows, :]
        mixed[rows, :] = xin[rows, :].astype(F32) * (inverse * inverse * inverse)

    loop(TILES, prepare)
    await_sums(1)
    fin[1] = total(1) / D

    def finish(i):
        rows = aligned(i, LEN)
        outv[rows, :] = (acc[rows, :] - mixed[rows, :] * column(fin[1, pl.ds(i, 1), :])).astype(BF16)

    loop(TILES, finish)
    store = local(outv, out_h, 7)
    store.start()

    for copy, cond in started:
        if cond is None:
            copy.wait_send()
        else:
            pl.when(cond)(copy.wait_send)
    for step in (1, 2, 3):
        for side, src_k, have, more in (
            (0, k - step, k >= step, k < 3),
            (1, k + step, k + step <= 3, k > 0),
        ):
            def drain(side=side, src_k=src_k, more=more):
                if step < 3:
                    pl.when(more)(line_copy(src_k, side, step).wait_send)
                sib_copy(src_k, step).wait_send()

            when(have, drain)
    def drain_chain(n):
        j, c = target(n // 3), n % 3
        sib_part(j, c, sib).wait_send()
        when(j > k, chain_copy(j, c, 0).wait_send)
        when(j < k, chain_copy(j, c, 1).wait_send)

    loop(12, drain_chain)
    store.wait()


def on_device(
    grad_out, block_input, norm_gain, queries, keys, values, filters, doc_starts, in_weight, out_weight
):
    hbm = pl.BlockSpec(memory_space=pl.ANY)
    vmem = pl.BlockSpec(memory_space=pltpu.VMEM)
    dma = pltpu.SemaphoreType.DMA
    return pl.pallas_call(
        kernel,
        out_shape=jax.ShapeDtypeStruct((TOK, CH), BF16),
        in_specs=[hbm, hbm, vmem, hbm, hbm, hbm, vmem, vmem, hbm, hbm],
        out_specs=hbm,
        scratch_shapes=[
            pltpu.VMEM((8, TOK, CH), BF16),
            pltpu.VMEM((3, 2, 4, 4, 128, CH), BF16),
            pltpu.VMEM((2, 4, 4, CH, 128), BF16),
            pltpu.VMEM((TOK, CH), BF16),
            pltpu.VMEM((TOK, CH), BF16),
            pltpu.VMEM((TOK, CH), BF16),
            pltpu.VMEM((TOK, CH), BF16),
            pltpu.VMEM((TOK + LEN, CH), BF16),
            pltpu.VMEM((TOK + LEN, CH), BF16),
            pltpu.VMEM((TOK, CH), F32),
            pltpu.VMEM((TOK, CH), F32),
            pltpu.VMEM((3, TOK, CH), BF16),
            pltpu.VMEM((32, LEN, 2 * LEN), BF16),
            pltpu.VMEM((32, LEN, 2 * LEN), BF16),
            pltpu.VMEM((2, 32, 2 * LEN), F32),
            pltpu.VMEM((LEN, 2 * LEN), BF16),
            pltpu.VMEM((3, 8, 2 * LEN), jnp.int32),
            pltpu.VMEM((2, 4, TOK, CH), BF16),
            pltpu.VMEM((4, TOK, CH), BF16),
            pltpu.VMEM((8, TOK, CH), BF16),
            pltpu.VMEM((2, 8, 8, 128), F32),
            pltpu.VMEM((2, 8, 128), F32),
            pltpu.VMEM((TOK, CH), BF16),
            dma((8,)),
            dma((2, 3)),
            dma((4,)),
            dma((4,)),
            dma((4,)),
            dma((2,)),
            dma((2,)),
            dma((2, 2, 4, 6)),
            dma((2, 2, 4, 6)),
            dma((4,)),
            dma((4,)),
            dma((2, 8)),
            dma((2, 8)),
            dma((4, 3)),
            dma((4, 3)),
            dma((4, 3)),
            dma((8, 3)),
        ],
        compiler_params=pltpu.CompilerParams(
            collective_id=0, has_side_effects=True, vmem_limit_bytes=66 * 1024 * 1000
        ),
    )(
        grad_out,
        block_input,
        norm_gain.reshape(1, -1),
        queries,
        keys,
        values,
        filters,
        doc_starts,
        jnp.transpose(in_weight, (1, 0, 2)),
        out_weight,
    )


def solution(mesh):
    placed = (
        P("ctx", "ch"),
        P("ctx", "ch"),
        P("ch"),
        P("ctx", "ch"),
        P("ctx", "ch"),
        P("ctx", "ch"),
        P("ch", None),
        P("ctx", None),
        P("ctx", None, "ch"),
        P("ch", "ctx"),
    )
    return jax.shard_map(
        on_device, mesh=mesh, in_specs=placed, out_specs=P("ctx", "ch"), check_vma=False
    )
```

```python
import functools

import jax
import jax.numpy as jnp
from jax import lax
from jax.experimental import pallas as pl
from jax.experimental.pallas import tpu as pltpu
from jax.sharding import PartitionSpec as P

D = 4096
LEN = 128
GROUP = 16
DOCS = 4
EPS = 1e-05
TOK = 768
CH = 512
TILES = TOK // LEN
BLOCKS = CH // 128
STACK = 128 // GROUP
F32 = jnp.float32
BF16 = jnp.bfloat16
NT = (((1,), (1,)), ((), ()))
SCHEDULE = (
    "a1", "b1", "a2", "b2", "a3", "b3", "F35", "c0", "a4", "c1", "b4", "d0",
    "a5", "c2", "Z01", "d1", "c3", "Z02", "d2", "c4", "T", "Z03", "d3", "F12",
    "F0", "Z11", "c5", "Z12", "d4", "c6", "a6", "b5", "M0", "Z13", "Z21", "B01",
    "Z22", "M1", "d5", "Z23", "B23", "M2", "B44", "b6", "B5", "d6",
)
STRIPS = ((0, 384), (384, 256), (640, 128))


def aligned(index, size):
    return pl.ds(index * size if isinstance(index, int) else pl.multiple_of(index * size, size), size)


def loop(count, body, start=0):
    def step(index, carry):
        body(index)
        return carry

    lax.fori_loop(start, count, step, 0)


def kernel(
    go_h, x_h, gain_v, q_h, k_h, v_h, filt_v, docs_v, iw_h, ow_h, out_h,
    grads, wts, ows, xin, qry, key, val, prod, wg, mixed, acc, stk, tabf, tabb, base, mask,
    docs, parts, sibs, runs, sums, fin, outv,
    lsem, ags, agr, bs, br, p0s, p0r, ws, wr, hs, hr, us, ur, ss, sr, cs, cr,
):
    ctx = lax.axis_index("ctx")
    ch = lax.axis_index("ch")
    x = ctx % 4
    y = (ctx // 4) % 4
    z = ctx // 16
    k = ch // 2
    core = ch % 2
    sib = 2 * k + 1 - core
    started = []

    def local(src, dst, index):
        return pltpu.make_async_copy(src, dst, lsem.at[index])

    def remote(src, dst, send, recv, to_ctx, to_ch):
        return pltpu.make_async_remote_copy(
            src, dst, send, recv, device_id=(to_ctx, to_ch), device_id_type=pl.DeviceIdType.MESH
        )

    def go(copy, cond=None):
        if cond is None:
            copy.start()
        else:
            pl.when(cond)(copy.start)
        started.append((copy, cond))

    def when(cond, body):
        pl.when(cond)(body)

    loads = [
        local(k_h, key, 0),
        local(v_h, val, 1),
        local(iw_h, wts.at[:, z, y, x], 2),
        local(ow_h, ows.at[z, y, x], 3),
        local(go_h, grads.at[ch], 4),
        local(x_h, xin, 5),
        local(q_h, qry, 6),
    ]
    for load in loads:
        load.start()

    barrier = pltpu.get_barrier_semaphore()
    up = (ctx + 1) % 32
    down = (ctx + 31) % 32

    def plane(dy, dx):
        return z * 16 + ((y + dy) % 4) * 4 + (x + dx) % 4

    partner = (1 - z) * 16 + y * 4 + x
    greet = [plane(0, 1), plane(0, 3), plane(1, 0), plane(3, 0), partner, up, down]
    for peer in greet:
        pl.semaphore_signal(barrier, inc=1, device_id=(peer, ch), device_id_type=pl.DeviceIdType.MESH)
    for step in range(1, 8):
        pl.semaphore_signal(
            barrier, inc=1, device_id=(ctx, (ch + step) % 8), device_id_type=pl.DeviceIdType.MESH
        )
    wide_row = lax.broadcasted_iota(jnp.int32, (8, 2 * LEN), 0)
    own = jnp.zeros((8, 2 * LEN), jnp.int32)
    for i in range(DOCS):
        own = jnp.where(wide_row == i, docs_v[0:1, i : i + 1], own)
    docs[0] = own

    loads[0].wait()
    loads[1].wait()

    def product(i):
        rows = aligned(i, LEN)
        prod[pl.ds(pl.multiple_of(i * LEN + LEN, LEN), LEN), :] = (
            key[rows, :].astype(F32) * val[rows, :].astype(F32)
        ).astype(BF16)

    loop(TILES, product)

    taps = filt_v[...]
    flip_row = lax.broadcasted_iota(jnp.int32, (LEN, 2 * LEN), 0)
    flip_col = lax.broadcasted_iota(jnp.int32, (LEN, 2 * LEN), 1)
    flip = jnp.where(flip_row + flip_col == LEN, 1.0, 0.0).astype(BF16)
    base[0] = jnp.dot(taps, flip, preferred_element_type=F32)
    base[1] = jnp.concatenate([taps.astype(F32), jnp.zeros((32, LEN), F32)], axis=1)

    def build(which, tab):
        def one(g):
            row = jnp.broadcast_to(base[which, pl.ds(g, 1), :], (LEN, 2 * LEN))
            tab[g] = pltpu.roll(row, 0, 1, stride=1, stride_axis=0).astype(BF16)

        loop(BLOCKS * STACK, one)

    build(0, tabf)

    loads[5].wait()

    def row_sums(i, which, wide):
        narrow = wide[:, 0:128] + wide[:, 128:256] + wide[:, 256:384] + wide[:, 384:512]
        sums[which, ch, pl.ds(i, 1), :] = jnp.sum(narrow.T, axis=0, keepdims=True)

    sums[0, ch] = jnp.zeros((8, 128), F32)
    sums[1, ch] = jnp.zeros((8, 128), F32)

    def squares(i):
        block = xin[aligned(i, LEN), :].astype(F32)
        row_sums(i, 0, block * block)

    loop(TILES, squares)

    pl.semaphore_wait(barrier, len(greet) + 7)

    def piece(w, zi, yi, xi, quarter):
        if w == 0:
            return ows.at[zi, yi, xi, pl.ds(quarter * 128, 128), :]
        return wts.at[:, zi, yi, xi, pl.ds(quarter * 32, 32), :]

    def ring_copy(w, zz, quarter, step):
        zi = z if zz == 0 else 1 - z
        shift = 3 if quarter % 2 == 0 else 1
        along_y = (quarter < 2) == (step < 3)
        hop = 1 if quarter % 2 == 0 else 3
        peer = plane(hop, 0) if along_y else plane(0, hop)
        if step < 3:
            back = shift * step
            yi = (y + back) % 4 if along_y else y
            xi = x if along_y else (x + back) % 4
            dst = piece(w, zi, yi, xi, quarter)
            src = dst
            if step == 0 and zz == 0:
                if w == 0:
                    src = ow_h.at[pl.ds(quarter * 128, 128), :]
                else:
                    src = iw_h.at[:, pl.ds(quarter * 32, 32), :]
        else:
            back = shift * (step - 3)
            if along_y:
                yi, xi = (y + back) % 4, slice(None)
            else:
                yi, xi = slice(None), (x + back) % 4
            dst = piece(w, zi, yi, xi, quarter)
            src = dst
        return remote(src, dst, ws.at[w, zz, quarter, step], wr.at[w, zz, quarter, step], peer, ch)

    def ring_arrival(w, zz, quarter, step):
        zi = z if zz == 0 else 1 - z
        shift = 3 if quarter % 2 == 0 else 1
        along_y = (quarter < 2) == (step < 3)
        back = shift * (step % 3 + 1)
        if step < 3:
            yi = (y + back) % 4 if along_y else y
            xi = x if along_y else (x + back) % 4
        elif along_y:
            yi, xi = (y + back) % 4, slice(None)
        else:
            yi, xi = slice(None), (x + back) % 4
        dst = piece(w, zi, yi, xi, quarter)
        return remote(dst, dst, ws.at[w, zz, quarter, step], wr.at[w, zz, quarter, step], ctx, ch)

    def swap_copy(w):
        if w == 0:
            return remote(ow_h, ows.at[z, y, x], p0s.at[0], p0r.at[0], partner, ch)
        return remote(iw_h, wts.at[:, z, y, x], p0s.at[1], p0r.at[1], partner, ch)

    def swap_arrival(w):
        dst = ows.at[1 - z, y, x] if w == 0 else wts.at[:, 1 - z, y, x]
        return remote(dst, dst, p0s.at[w], p0r.at[w], ctx, ch)

    def weights(w, zz, event):
        if event == 0 and zz == 1:
            swap_arrival(w).wait_recv()
        if event == 3 and zz == 0:
            loads[3 - w].wait()
        for quarter in range(4):
            if event >= 1:
                ring_arrival(w, zz, quarter, event - 1).wait_recv()
            if event <= 5:
                go(ring_copy(w, zz, quarter, event))

    def strip(t):
        return pl.ds(*STRIPS[t])

    def line_copy(src_k, side, step, t):
        d = 2 * src_k + core
        to = (ch + 2) % 8 if side == 0 else (ch + 6) % 8
        dst = grads.at[d, strip(t)]
        src = go_h.at[strip(t)] if step == 0 else dst
        return remote(src, dst, ags.at[side, step, t], agr.at[src_k, t], ctx, to)

    def sib_copy(src_k, step, t):
        dst = grads.at[2 * src_k + core, strip(t)]
        src = go_h.at[strip(t)] if step == 0 else dst
        return remote(src, dst, bs.at[src_k, t], br.at[src_k, t], ctx, sib)

    sides = ((0, k, k < 3), (1, 3 - k, k > 0))

    def line_relay(t, step):
        for side, behind, more in sides:
            src_k = k - step + 2 * step * side

            def relay(side=side, behind=behind, more=more, src_k=src_k):
                dst = grads.at[2 * src_k + core, strip(t)]
                remote(dst, dst, ags.at[side, step, t], agr.at[src_k, t], ctx, ch).wait_recv()
                if step < 3:
                    pl.when(more)(line_copy(src_k, side, step, t).start)
                sib_copy(src_k, step, t).start()
                if t < 2:
                    pl.when(more & (behind == step))(line_copy(k, side, 0, t + 1).start)

            when(behind >= step, relay)

    def multiply(t):
        rows = strip(t)
        for src_k in range(4):
            dst = grads.at[2 * src_k + 1 - core, rows]
            remote(dst, dst, bs.at[src_k, t], br.at[src_k, t], ctx, ch).wait_recv()

        def one(i):
            d = (ch + i) % 8
            zi, yi = d // 4, d % 4
            wide = jnp.concatenate([ows[zi, yi, xi] for xi in range(4)], axis=1)
            acc[rows, :] = acc[rows, :] + lax.dot_general(
                grads[d, rows, :], wide, NT, preferred_element_type=F32
            )

        loop(8, one)

    go(remote(docs.at[0], docs.at[1], hs.at[0], hr.at[0], up, ch))
    go(remote(docs.at[0], docs.at[2], hs.at[1], hr.at[1], down, ch))
    weights(0, 0, 0)
    weights(1, 0, 0)
    go(remote(prod.at[pl.ds(TOK, LEN), :], prod.at[pl.ds(0, LEN), :], hs.at[2], hr.at[2], up, ch))
    go(swap_copy(0))
    go(swap_copy(1))
    for side, behind, more in sides:
        when(more, line_copy(k, side, 0, 0).start)
        for t in (1, 2):
            when(behind == 0, line_copy(k, side, 0, t).start)
    for t in range(3):
        go(sib_copy(k, 0, t))

    def send_sums(which):
        for step in range(1, 8):
            to = (ch + step) % 8
            go(remote(sums.at[which, ch], sums.at[which, ch], us.at[which, step], ur.at[which, step], ctx, to))

    def await_sums(which):
        for step in range(1, 8):
            src = (ch + 8 - step) % 8
            remote(
                sums.at[which, src], sums.at[which, src], us.at[which, step], ur.at[which, step], ctx, ch
            ).wait_recv()

    send_sums(0)

    lane_group = lax.broadcasted_iota(jnp.int32, (LEN, 128), 1) // GROUP
    row_pos = lax.broadcasted_iota(jnp.int32, (LEN, 2 * LEN), 0)
    col_pos = lax.broadcasted_iota(jnp.int32, (LEN, 2 * LEN), 1)

    def set_mask(source, target, starts):
        cut = jnp.zeros((LEN, 2 * LEN), F32)
        for first in starts:
            cut = jnp.where((source < first) & (first <= target), 1.0, cut)
        mask[...] = (1.0 - cut).astype(BF16)

    def convolve(tab, src, i, b):
        lanes = aligned(b, 128)
        first = i * LEN if isinstance(i, int) else pl.multiple_of(i * LEN, LEN)
        block = src[pl.ds(first, 2 * LEN), lanes]
        left = (tab[pl.ds(pl.multiple_of(b * STACK, STACK), STACK)] * mask[...][None]).reshape(
            STACK * LEN, 2 * LEN
        )
        every = jnp.dot(left, block, preferred_element_type=F32).reshape(STACK, LEN, 128)
        picked = every[0]
        for g in range(1, STACK):
            picked = jnp.where(lane_group == g, every[g], picked)
        return picked

    def forward(i):
        firsts = [docs[0, r : r + 1, :] for r in range(DOCS)]
        if isinstance(i, int):
            firsts.append(docs[1, DOCS - 1 : DOCS, :] - TOK)
        set_mask(col_pos + (i * LEN - LEN), row_pos + i * LEN, firsts)

        def one(b):
            mixed[aligned(i, LEN), aligned(b, 128)] = convolve(tabf, prod, i, b)

        loop(BLOCKS, one)

    def gates(i):
        rows = aligned(i, LEN)
        mix = acc[rows, :]
        wg[rows, :] = (mix * qry[rows, :].astype(F32)).astype(BF16)
        stk[0, rows, :] = (mix * mixed[rows, :]).astype(BF16)

    def head_copy(to):
        return remote(wg.at[pl.ds(0, LEN), :], wg.at[pl.ds(TOK, LEN), :], hs.at[3], hr.at[3], to, ch)

    def backward(i):
        firsts = [docs[0, r : r + 1, :] for r in range(DOCS)]
        if isinstance(i, int):
            firsts += [docs[2, r : r + 1, :] + TOK for r in range(DOCS)]
        set_mask(row_pos + i * LEN, col_pos + i * LEN, firsts)

        def one(b):
            rows, lanes = aligned(i, LEN), aligned(b, 128)
            conv = convolve(tabb, wg, i, b)
            stk[1, rows, lanes] = (conv * val[rows, lanes].astype(F32)).astype(BF16)
            stk[2, rows, lanes] = (conv * key[rows, lanes].astype(F32)).astype(BF16)

        loop(BLOCKS, one)

    order = [3 * (1 - k // 2), (2 + 3 * k) % 5, 1 + k % 2, k]

    def target(pos):
        return sum(order[i] * ((4 - (pos + 4 - i) % 4) // 4) for i in range(4))

    def chunk(c):
        return aligned(c, 256)

    def sib_part(j, c, to):
        rows = chunk(c)
        return remote(parts.at[0, j, rows], sibs.at[j, rows], ss.at[j, c], sr.at[j, c], ctx, to)

    def run_arrival(slot, c):
        rows = chunk(c)
        remote(runs.at[slot, rows], runs.at[slot, rows], cs.at[0, c], cr.at[slot, c], ctx, ch).wait_recv()

    def chain_copy(j, c, side):
        rows = chunk(c)
        to = (ch + 2) % 8 if side == 0 else (ch + 6) % 8
        slot = j + 4 * side
        return remote(parts.at[1, j, rows], runs.at[slot, rows], cs.at[j, c], cr.at[slot, c], ctx, to)

    def partials(j, c):
        rows = chunk(c)

        def one(part):
            d = 2 * j + (1 - core) * (1 - part) + core * part
            zi, yi = d // 4, d % 4
            total = lax.dot_general(
                stk[0, rows, :], wts[0, zi, yi].reshape(CH, CH), NT, preferred_element_type=F32
            )
            for b in (1, 2):
                total = total + lax.dot_general(
                    stk[b, rows, :], wts[b, zi, yi].reshape(CH, CH), NT, preferred_element_type=F32
                )
            parts[part, j, rows, :] = total.astype(BF16)
            when(part == 0, sib_part(j, c, sib).start)

        loop(2, one)

    def forward_sum(j, c):
        sib_part(j, c, ch).wait_recv()
        inner = (k == 1) | (k == 2)
        slot = j + 4 * ((k - j + 3) // 4)

        def pieces(i):
            return pl.ds(pl.multiple_of(c * 256 + i * 64, 64), 64)

        def with_run():
            run_arrival(slot, c)

            def add(i):
                rows = pieces(i)
                parts[1, j, rows, :] = (
                    parts[1, j, rows, :].astype(F32)
                    + sibs[j, rows, :].astype(F32)
                    + runs[slot, rows, :].astype(F32)
                ).astype(BF16)

            loop(4, add)

        def without_run():
            def add(i):
                rows = pieces(i)
                parts[1, j, rows, :] = (
                    parts[1, j, rows, :].astype(F32) + sibs[j, rows, :].astype(F32)
                ).astype(BF16)

            loop(4, add)

        when(inner, with_run)
        when(jnp.logical_not(inner), without_run)
        when(j > k, chain_copy(j, c, 0).start)
        when(j < k, chain_copy(j, c, 1).start)

    def clear(slot):
        def one():
            runs[slot] = jnp.zeros((TOK, CH), BF16)

        return one

    when(k == 0, clear(0))
    when(k == 3, clear(7))

    loads[4].wait()
    loads[6].wait()
    acc[...] = jnp.zeros((TOK, CH), F32)

    def act(name):
        kind, args = name[0], [int(c) for c in name[1:]]
        if kind in "abcd":
            weights("abcd".index(kind) % 2, "abcd".index(kind) // 2, args[0])
        elif kind == "Z":
            line_relay(*args)
        elif kind == "M":
            multiply(args[0])
            first, count = STRIPS[args[0]]
            loop((first + count) // LEN, gates, first // LEN)
            if args[0] == 0:
                go(head_copy(down))
        elif kind == "F":
            if args[0] == 0:
                halo.wait_recv()
                remote(docs.at[0], docs.at[1], hs.at[0], hr.at[0], ctx, ch).wait_recv()
                forward(0)
            else:
                loop(args[1] + 1, forward, args[0])
        elif kind == "T":
            build(1, tabb)
        elif kind == "B":
            if args[0] == 5:
                head_copy(ctx).wait_recv()
                remote(docs.at[0], docs.at[2], hs.at[1], hr.at[1], ctx, ch).wait_recv()
                backward(5)
            else:
                loop(args[1] + 1, backward, args[0])

    halo = remote(prod.at[pl.ds(TOK, LEN), :], prod.at[pl.ds(0, LEN), :], hs.at[2], hr.at[2], ctx, ch)
    for name in SCHEDULE:
        act(name)

    def job(n):
        partials(target(n // 3), n % 3)
        done = n - 1

        def behind():
            forward_sum(target(done // 3), done % 3)

        when((done >= 0) & (done < 9), behind)

    loop(12, job)

    def total(which):
        full = sums[which, 0]
        for src in range(1, 8):
            full = full + sums[which, src]
        return full

    def column(row):
        tall = jnp.broadcast_to(row, (128, 128)).T
        return jnp.concatenate([tall] * BLOCKS, axis=1)

    await_sums(0)
    fin[0] = lax.rsqrt(total(0) / D + EPS)
    gain = gain_v[...].astype(F32)

    def cross(i):
        rows = aligned(i, LEN)
        norm = (
            parts[1, k, rows, :].astype(F32)
            + sibs[k, rows, :].astype(F32)
            + runs[k, rows, :].astype(F32)
            + runs[4 + k, rows, :].astype(F32)
        )
        scaled = gain * norm
        acc[rows, :] = scaled
        row_sums(i, 1, scaled * xin[rows, :].astype(F32))

    for c in range(3):
        sib_part(k, c, ch).wait_recv()
        when(k > 0, functools.partial(run_arrival, k, c))
        when(k < 3, functools.partial(run_arrival, 4 + k, c))
        loop(2 * c + 2, cross, 2 * c)
    send_sums(1)

    def prepare(i):
        rows = aligned(i, LEN)
        inverse = column(fin[0, pl.ds(i, 1), :])
        acc[rows, :] = grads[ch, rows, :].astype(F32) + inverse * acc[rows, :]
        mixed[rows, :] = xin[rows, :].astype(F32) * (inverse * inverse * inverse)

    loop(TILES, prepare)
    await_sums(1)
    fin[1] = total(1) / D

    def finish(i):
        rows = aligned(i, LEN)
        outv[rows, :] = (acc[rows, :] - mixed[rows, :] * column(fin[1, pl.ds(i, 1), :])).astype(BF16)

    loop(TILES, finish)
    store = local(outv, out_h, 7)
    store.start()

    for copy, cond in started:
        if cond is None:
            copy.wait_send()
        else:
            pl.when(cond)(copy.wait_send)
    for t in range(3):
        for side, behind, more in sides:
            when(more, line_copy(k, side, 0, t).wait_send)
            for step in (1, 2, 3):
                src_k = k - step + 2 * step * side

                def drain(side=side, more=more, src_k=src_k, step=step):
                    if step < 3:
                        pl.when(more)(line_copy(src_k, side, step, t).wait_send)
                    sib_copy(src_k, step, t).wait_send()

                when(behind >= step, drain)

    def drain_chain(n):
        j, c = n // 3, n % 3
        sib_part(j, c, sib).wait_send()
        when(j > k, chain_copy(j, c, 0).wait_send)
        when(j < k, chain_copy(j, c, 1).wait_send)

    loop(12, drain_chain)
    store.wait()


def on_device(
    grad_out, block_input, norm_gain, queries, keys, values, filters, doc_starts, in_weight, out_weight
):
    hbm = pl.BlockSpec(memory_space=pl.ANY)
    vmem = pl.BlockSpec(memory_space=pltpu.VMEM)
    dma = pltpu.SemaphoreType.DMA
    return pl.pallas_call(
        kernel,
        out_shape=jax.ShapeDtypeStruct((TOK, CH), BF16),
        in_specs=[hbm, hbm, vmem, hbm, hbm, hbm, vmem, vmem, hbm, hbm],
        out_specs=hbm,
        scratch_shapes=[
            pltpu.VMEM((8, TOK, CH), BF16),
            pltpu.VMEM((3, 2, 4, 4, 128, CH), BF16),
            pltpu.VMEM((2, 4, 4, CH, 128), BF16),
            pltpu.VMEM((TOK, CH), BF16),
            pltpu.VMEM((TOK, CH), BF16),
            pltpu.VMEM((TOK, CH), BF16),
            pltpu.VMEM((TOK, CH), BF16),
            pltpu.VMEM((TOK + LEN, CH), BF16),
            pltpu.VMEM((TOK + LEN, CH), BF16),
            pltpu.VMEM((TOK, CH), F32),
            pltpu.VMEM((TOK, CH), F32),
            pltpu.VMEM((3, TOK, CH), BF16),
            pltpu.VMEM((32, LEN, 2 * LEN), BF16),
            pltpu.VMEM((32, LEN, 2 * LEN), BF16),
            pltpu.VMEM((2, 32, 2 * LEN), F32),
            pltpu.VMEM((LEN, 2 * LEN), BF16),
            pltpu.VMEM((3, 8, 2 * LEN), jnp.int32),
            pltpu.VMEM((2, 4, TOK, CH), BF16),
            pltpu.VMEM((4, TOK, CH), BF16),
            pltpu.VMEM((8, TOK, CH), BF16),
            pltpu.VMEM((2, 8, 8, 128), F32),
            pltpu.VMEM((2, 8, 128), F32),
            pltpu.VMEM((TOK, CH), BF16),
            dma((8,)),
            dma((2, 3, 3)),
            dma((4, 3)),
            dma((4, 3)),
            dma((4, 3)),
            dma((2,)),
            dma((2,)),
            dma((2, 2, 4, 6)),
            dma((2, 2, 4, 6)),
            dma((4,)),
            dma((4,)),
            dma((2, 8)),
            dma((2, 8)),
            dma((4, 3)),
            dma((4, 3)),
            dma((4, 3)),
            dma((8, 3)),
        ],
        compiler_params=pltpu.CompilerParams(
            collective_id=0, has_side_effects=True, vmem_limit_bytes=66 * 1024 * 1000
        ),
    )(
        grad_out,
        block_input,
        norm_gain.reshape(1, -1),
        queries,
        keys,
        values,
        filters,
        doc_starts,
        jnp.transpose(in_weight, (1, 0, 2)),
        out_weight,
    )


def solution(mesh):
    placed = (
        P("ctx", "ch"),
        P("ctx", "ch"),
        P("ch"),
        P("ctx", "ch"),
        P("ctx", "ch"),
        P("ctx", "ch"),
        P("ch", None),
        P("ctx", None),
        P("ctx", None, "ch"),
        P("ch", "ctx"),
    )
    return jax.shard_map(
        on_device, mesh=mesh, in_specs=placed, out_specs=P("ctx", "ch"), check_vma=False
    )
```
